256 devices in a mesh: energy: 128 (over y_lo, x, z, core), mode: 2 (over y_hi).
Axes of the slice: x: 4, y: 4 (y_hi: 2, y_lo: 2; y = y_hi * 2 + y_lo), z: 8, core: 2. Of those that a mesh axis runs over, the one named last changes fastest.
Arguments:
- spectral: float32 [128, 896, 896], P('energy', 'mode'), may hold values from -6 to 6
- coupling: bfloat16 [2, 896, 896], P('mode'), may hold values from -0.1875 to 0.1875
- offsets: int32 [2], P('mode'), may hold values from 1 to 2, as said below
- occupation: int32 [2, 128], P('mode', 'energy'), may hold values from 0 to 3
Outputs:
- self_energy: float32 [128, 896, 896], P('energy', 'mode')
The draws below stay inside these ranges and needn't reach their ends.
Inputs may be any that keep to these rules, and one draw needn't show every extreme that they name: `offsets`: each offset from 1 to 2 belongs to exactly 1 modes.
All inputs are finite; a program needn't handle non-finite values.
Results may differ from the reference program's by a relative error of at most 0.0041.
Values sent between devices are 32-bit elements; how exact they have to be, the bound alone decides.
A program may use at most 64 MiB of HBM per device.

```python
import jax
import jax.numpy as jnp
from jax import lax

NORB = 896
KMAX = 2
ENERGIES = 128
MODES = 2


def draw_offsets(key, part):
    shuffled = jax.random.permutation(jax.random.fold_in(key, 11), MODES)
    return (1 + shuffled % KMAX).astype(jnp.int32)


def with_ends(drawn, key, low, top_value):
    spot = [jax.random.randint(jax.random.fold_in(key, axis), (), 0, length) for axis, length in enumerate(drawn.shape)]
    longest = drawn.shape.index(max(drawn.shape))
    beside = spot[:longest] + [(spot[longest] + 1) % drawn.shape[longest]] + spot[longest + 1:]
    return drawn.at[tuple(spot)].set(low).at[tuple(beside)].set(top_value)


def block_levels(key, extent, cuts, low, high):
    level = 1.0
    for position, parts in cuts:
        steps = jax.random.uniform(jax.random.fold_in(jax.random.fold_in(key, 6), position), (parts,), jnp.float32, low / len(cuts), high / len(cuts))
        level = level * jnp.repeat(jnp.exp(steps), extent[position] // parts).reshape((-1,) + (1,) * (len(extent) - 1 - position))
    return level


def normal_values(stream_key, dims, deviation, bound, shards=(), kind=jnp.bfloat16):
    entries = jax.random.normal(stream_key, dims, jnp.float32) * deviation
    if len(shards) > 0:
        entries = block_levels(stream_key, dims, shards, -0.22, 0.18) * entries
    return jnp.clip(entries, min=-bound, max=bound).astype(kind)


def setup_inputs(seed: int = 0) -> dict:
    keys = jax.random.split(jax.random.key(seed), 5)
    spectral = normal_values(keys[0], (ENERGIES, NORB, NORB), 1.0, 6.0, ((0, 128), (1, 2)), jnp.float32)
    coupling = normal_values(keys[1], (MODES, NORB, NORB), NORB ** -0.5, 0.1875, ((0, 2),))
    offsets = draw_offsets(jax.random.fold_in(keys[4], 71), 0)
    occupation = with_ends(jax.random.randint(keys[3], (MODES, ENERGIES), 0, 4), jax.random.fold_in(keys[3], 1), 0, 3).astype(jnp.int32)
    return dict(spectral=spectral, coupling=coupling, offsets=offsets, occupation=occupation)


def reference(spectral, coupling, offsets, occupation):
    energies = spectral.shape[0]
    padded = jnp.pad(spectral, ((KMAX, KMAX), (0, 0), (0, 0)))
    energy_index = jnp.arange(energies, dtype=jnp.int32)

    def one_mode(running, inputs):
        matrix, offset, occupied = inputs
        emitted = jnp.take(padded, energy_index + KMAX - offset, axis=0)
        absorbed = jnp.take(padded, energy_index + KMAX + offset, axis=0)
        emission = (occupied + 1).astype(jnp.float32)[:, None, None]
        absorption = occupied.astype(jnp.float32)[:, None, None]
        combined = (emission * emitted + absorption * absorbed).astype(jnp.bfloat16)
        matrix_wide = matrix.astype(jnp.float32)
        coupled = jnp.einsum("ij,ejk->eik", matrix_wide, combined.astype(jnp.float32)).astype(jnp.bfloat16)
        mode_term = jnp.einsum("eik,lk->eil", coupled.astype(jnp.float32), matrix_wide)
        return running + mode_term, None

    start_value = jnp.zeros(spectral.shape, jnp.float32)
    running, unused = lax.scan(one_mode, start_value, (coupling, offsets, occupation))
    return running / MODES
```

```python
import functools

import jax
import jax.numpy as jnp
from jax import lax
from jax.experimental import pallas as pl
from jax.experimental.pallas import tpu as pltpu
from jax.sharding import PartitionSpec as P

MESH = pl.DeviceIdType.MESH
CORES, ALONG_Z, ALONG_X = 2, 8, 4
CHUNK = 64
F32, BF16 = jnp.float32, jnp.bfloat16


def dot_nt(a, b):
    return lax.dot_general(a, b, (((1,), (1,)), ((), ())), preferred_element_type=F32)


def dot_nn(a, b):
    return jnp.dot(a, b, preferred_element_type=F32)


def kernel(
    energies,
    x_ref,
    g_ref,
    off_ref,
    occ_ref,
    o_ref,
    near,
    g_mine,
    g_slice,
    g_got,
    g_other,
    cols,
    coupled,
    p_out,
    p_in,
    occ_mine,
    occ_got,
    load_sem,
    near_send,
    near_recv,
    fwd_send,
    fwd_recv,
    sib_send,
    sib_recv,
    g_send,
    g_recv,
    occ_send,
    occ_recv,
    p_send,
    p_recv,
):
    e = lax.axis_index("energy")
    m = lax.axis_index("mode")
    rows, norb = x_ref.shape[1], x_ref.shape[2]
    chunks = rows // CHUNK
    core = e % CORES
    x_at = (e // (CORES * ALONG_Z)) % ALONG_X
    slices = CORES * ALONG_X
    depth = norb // slices
    up = (lax.rem(e + 2, energies), m)
    down = (lax.rem(e + energies - 2, energies), m)
    sibling = (e + 1 - 2 * core, m)
    partner = (e, 1 - m)
    across = (lax.rem(e + energies // 2, energies), 1 - m)
    x_peers = []
    for step in range(1, ALONG_X):
        there = lax.rem(x_at + step, ALONG_X)
        x_peers.append((e + (there - x_at) * (CORES * ALONG_Z), m))

    load = pltpu.make_async_copy(g_ref.at[0], g_mine, load_sem)
    load.start()
    barrier = pltpu.get_barrier_semaphore()
    greeted = [up, down, sibling, partner, across, *x_peers]
    for device in greeted:
        pl.semaphore_signal(barrier, inc=1, device_id=device, device_id_type=MESH)
    pl.semaphore_wait(barrier, len(greeted))

    def remote(src, dst, send, recv, device):
        return pltpu.make_async_remote_copy(
            src_ref=src, dst_ref=dst, send_sem=send, recv_sem=recv, device_id=device, device_id_type=MESH
        )

    def at(i, base=0):
        return pl.ds(pl.multiple_of(base + i * CHUNK, CHUNK), CHUNK)

    def to_up(i):
        return remote(x_ref.at[0, at(i)], near.at[0, at(i)], near_send.at[0, i], near_recv.at[0, i], up)

    def to_down(i):
        return remote(x_ref.at[0, at(i)], near.at[1, at(i)], near_send.at[1, i], near_recv.at[1, i], down)

    def to_sibling(i):
        return remote(near.at[1 - core, at(i)], near.at[3, at(i)], fwd_send.at[i], fwd_recv.at[i], sibling)

    def to_partner(i):
        return remote(p_out.at[at(i)], p_in.at[at(i)], p_send.at[i], p_recv.at[i], partner)

    own_to_sibling = remote(x_ref.at[0], near.at[2], sib_send, sib_recv, sibling)

    @pl.loop(0, chunks)
    def _(i):
        to_up(i).start()
        to_down(i).start()

    own_to_sibling.start()

    my_slice = x_at * CORES + core
    load.wait()
    g_slice[...] = g_mine[pl.ds(pl.multiple_of(my_slice * depth, 16), depth), :].astype(F32)
    occ_mine[...] = jnp.full(occ_mine.shape, occ_ref[0, 0].astype(F32), F32)
    slice_across = remote(g_slice, g_got.at[my_slice], g_send.at[0], g_recv.at[0], across)
    slice_across.start()
    occ_copy = remote(occ_mine, occ_got, occ_send, occ_recv, partner)
    occ_copy.start()

    def own_columns(matrix):
        pick = lax.broadcasted_iota(jnp.int32, (norb, rows), 0) == (
            lax.broadcasted_iota(jnp.int32, (norb, rows), 1) + m * rows
        )
        return dot_nn(matrix, jnp.where(pick, 1.0, 0.0).astype(BF16)).astype(BF16)

    cols[0] = own_columns(g_mine[...])

    slice_across.wait_recv()
    spread = []
    for step in range(1, ALONG_X):
        copy = remote(
            g_got.at[my_slice], g_got.at[my_slice], g_send.at[step], g_recv.at[step], x_peers[step - 1]
        )
        copy.start()
        spread.append(copy)
    to_sib = [remote(g_got.at[my_slice], g_got.at[my_slice], g_send.at[4], g_recv.at[4], sibling)]
    to_sib[0].start()

    occ_copy.wait_recv()
    own_one = off_ref[0] == 1
    own_occ = occ_mine[0:1, 0:1]
    other_occ = occ_got[0:1, 0:1]
    one_sel = jnp.where(own_one, 1.0, 0.0)
    is_one = (one_sel, 1.0 - one_sel)
    low2 = jnp.where(e >= 2, 1.0, 0.0)
    high2 = jnp.where(e < energies - 2, 1.0, 0.0)
    on_core = core.astype(F32)
    third = jnp.where((e > 0) & (e < energies - 1), 1.0, 0.0)
    weights = []
    for occ, one in zip((own_occ, other_occ), is_one):
        weights.append(
            (
                (occ + 1.0) * ((1.0 - one) * low2),
                occ * ((1.0 - one) * high2),
                (occ + on_core) * one,
                (occ + (1.0 - on_core)) * (one * third),
            )
        )

    own_to_sibling.wait_recv()

    def take_chunk(i):
        to_up(i).wait_recv()
        to_down(i).wait_recv()
        to_sibling(i).start()

    def couple(i, which, matrix):
        w = weights[which]
        combined = w[0] * near[0, at(i), :] + w[1] * near[1, at(i), :]
        combined = combined + (w[2] * near[2, at(i), :] + w[3] * near[3, at(i), :])
        coupled[which, at(i), :] = dot_nt(combined.astype(BF16), matrix[...]).astype(BF16)

    @pl.loop(0, chunks - 1)
    def _(i):
        take_chunk(i)
        to_sibling(i).wait_recv()
        couple(i, 0, g_mine)

    for step in range(1, ALONG_X):
        peer_slice = lax.rem(x_at + ALONG_X - step, ALONG_X) * CORES + core
        remote(
            g_got.at[peer_slice], g_got.at[peer_slice], g_send.at[step], g_recv.at[step], x_peers[step - 1]
        ).wait_recv()
        copy = remote(
            g_got.at[peer_slice], g_got.at[peer_slice], g_send.at[4 + step], g_recv.at[4 + step], sibling
        )
        copy.start()
        to_sib.append(copy)
    for step in range(ALONG_X):
        peer_slice = lax.rem(x_at + ALONG_X - step, ALONG_X) * CORES + 1 - core
        remote(
            g_got.at[peer_slice], g_got.at[peer_slice], g_send.at[4 + step], g_recv.at[4 + step], sibling
        ).wait_recv()
    for k in range(slices):
        g_other[k * depth : (k + 1) * depth, :] = g_got[k].astype(BF16)
    cols[1] = own_columns(g_other[...])

    @pl.loop(0, chunks - 1)
    def _(i):
        couple(i, 1, g_other)

    last = chunks - 1
    take_chunk(last)
    to_sibling(last).wait_recv()
    couple(last, 0, g_mine)
    couple(last, 1, g_other)

    def partial(i, base):
        there = at(i, base)
        return dot_nn(cols[0, there, :], coupled[0]) + dot_nn(cols[1, there, :], coupled[1])

    @pl.loop(0, chunks)
    def _(i):
        p_out[at(i), :] = partial(i, (1 - m) * rows)
        to_partner(i).start()

    @pl.loop(0, chunks)
    def _(i):
        o_ref[0, at(i), :] = partial(i, m * rows)

    @pl.loop(0, chunks)
    def _(i):
        to_partner(i).wait_recv()
        o_ref[0, at(i), :] = (o_ref[0, at(i), :] + p_in[at(i), :]) * 0.5

    @pl.loop(0, chunks)
    def _(i):
        to_up(i).wait_send()
        to_down(i).wait_send()
        to_sibling(i).wait_send()
        to_partner(i).wait_send()

    own_to_sibling.wait_send()
    slice_across.wait_send()
    occ_copy.wait_send()
    for copy in spread + to_sib:
        copy.wait_send()


def shards(energies, spectral, coupling, offsets, occupation):
    _, rows, norb = spectral.shape
    chunks = rows // CHUNK
    slices = CORES * ALONG_X
    dma = pltpu.SemaphoreType.DMA
    anywhere = pl.BlockSpec(memory_space=pltpu.HBM)
    scalar = pl.BlockSpec(memory_space=pltpu.SMEM)
    return pl.pallas_call(
        functools.partial(kernel, energies),
        out_shape=jax.ShapeDtypeStruct(spectral.shape, F32),
        in_specs=[anywhere, anywhere, scalar, scalar],
        out_specs=pl.BlockSpec(memory_space=pltpu.VMEM),
        scratch_shapes=[
            pltpu.VMEM((4, rows, norb), F32),
            pltpu.VMEM((norb, norb), BF16),
            pltpu.VMEM((norb // slices, norb), F32),
            pltpu.VMEM((slices, norb // slices, norb), F32),
            pltpu.VMEM((norb, norb), BF16),
            pltpu.VMEM((2, norb, rows), BF16),
            pltpu.VMEM((2, rows, norb), BF16),
            pltpu.VMEM((rows, norb), F32),
            pltpu.VMEM((rows, norb), F32),
            pltpu.VMEM((8, 128), F32),
            pltpu.VMEM((8, 128), F32),
            dma,
            dma((2, chunks)),
            dma((2, chunks)),
            dma((chunks,)),
            dma((chunks,)),
            dma,
            dma,
            dma((8,)),
            dma((8,)),
            dma,
            dma,
            dma((chunks,)),
            dma((chunks,)),
        ],
        compiler_params=pltpu.CompilerParams(
            collective_id=0, has_side_effects=True, vmem_limit_bytes=48 << 20
        ),
        name="born_step",
    )(spectral, coupling, offsets, occupation)


def solution(mesh):
    return jax.shard_map(
        functools.partial(shards, mesh.shape["energy"]),
        mesh=mesh,
        in_specs=(P("energy", "mode", None), P("mode", None, None), P("mode"), P("mode", "energy")),
        out_specs=P("energy", "mode", None),
        check_vma=False,
    )
```

```python
import functools

import jax
import jax.numpy as jnp
from jax import lax
from jax.experimental import pallas as pl
from jax.experimental.pallas import tpu as pltpu
from jax.sharding import PartitionSpec as P

MESH = pl.DeviceIdType.MESH
CORES, ALONG_Z, ALONG_X = 2, 8, 4
CHUNK = 64
LANES = 128
PIECE = 256
F32, BF16 = jnp.float32, jnp.bfloat16


def dot(a, b):
    return jnp.dot(a, b, preferred_element_type=F32)


def kernel(
    energies,
    x_ref,
    g_ref,
    off_ref,
    occ_ref,
    o_ref,
    near,
    g_mine,
    g_send_buf,
    g_got,
    turned,
    cols,
    coupled,
    p_out,
    p_in,
    occ_mine,
    occ_got,
    load_sem,
    near_send,
    near_recv,
    fwd_send,
    fwd_recv,
    sib_send,
    sib_recv,
    g_send,
    g_recv,
    occ_send,
    occ_recv,
    p_send,
    p_recv,
):
    e = lax.axis_index("energy")
    m = lax.axis_index("mode")
    rows, norb = x_ref.shape[1], x_ref.shape[2]
    chunks = rows // CHUNK
    core = e % CORES
    x_at = (e // (CORES * ALONG_Z)) % ALONG_X
    up = (lax.rem(e + 2, energies), m)
    down = (lax.rem(e + energies - 2, energies), m)
    sibling = (e + 1 - 2 * core, m)
    partner = (e, 1 - m)
    across = (lax.rem(e + energies // 2, energies), 1 - m)
    z_at = (e // CORES) % ALONG_Z
    way = jnp.where(z_at < ALONG_Z // 2, -1, 1)
    x_next = lax.rem(x_at + way + ALONG_X, ALONG_X)
    x_last = lax.rem(x_at - way + ALONG_X, ALONG_X)
    ring_next = (e + (x_next - x_at) * (CORES * ALONG_Z), m)
    ring_last = (e + (x_last - x_at) * (CORES * ALONG_Z), m)

    load = pltpu.make_async_copy(g_ref.at[0], g_mine, load_sem)
    load.start()
    barrier = pltpu.get_barrier_semaphore()
    greeted = [up, down, sibling, partner, across, ring_next, ring_last]
    for device in greeted:
        pl.semaphore_signal(barrier, inc=1, device_id=device, device_id_type=MESH)
    pl.semaphore_wait(barrier, len(greeted))

    def remote(src, dst, send, recv, device):
        return pltpu.make_async_remote_copy(
            src_ref=src, dst_ref=dst, send_sem=send, recv_sem=recv, device_id=device, device_id_type=MESH
        )

    def at(i, base=0):
        return pl.ds(pl.multiple_of(base + i * CHUNK, CHUNK), CHUNK)

    def rows_at(start):
        return pl.ds(pl.multiple_of(start, CHUNK), CHUNK)

    def to_up(i):
        return remote(x_ref.at[0, at(i)], near.at[0, at(i)], near_send.at[0, i], near_recv.at[0, i], up)

    def to_down(i):
        return remote(x_ref.at[0, at(i)], near.at[1, at(i)], near_send.at[1, i], near_recv.at[1, i], down)

    def to_sibling(i):
        return remote(near.at[1 - core, at(i)], near.at[3, at(i)], fwd_send.at[i], fwd_recv.at[i], sibling)

    def to_partner(k, j):
        return remote(p_out.at[:, j], p_in.at[:, j], p_send.at[k], p_recv.at[k], partner)

    own_to_sibling = remote(x_ref.at[0], near.at[2], sib_send, sib_recv, sibling)

    @pl.loop(0, chunks)
    def _(i):
        to_up(i).start()
        to_down(i).start()

    own_to_sibling.start()

    load.wait()
    half = core * rows
    mine = half + x_at * CHUNK
    g_send_buf[0:CHUNK, :] = g_mine[rows_at(mine), :].astype(F32)
    slice_across = remote(
        g_send_buf.at[pl.ds(0, CHUNK)], g_got.at[rows_at(mine)], g_send.at[0], g_recv.at[0], across
    )
    slice_across.start()
    occ_mine[...] = jnp.full(occ_mine.shape, occ_ref[0, 0].astype(F32), F32)
    occ_copy = remote(occ_mine, occ_got, occ_send, occ_recv, partner)
    occ_copy.start()
    ring_rows = ALONG_X * CHUNK
    direct_rows = rows - ring_rows
    direct = pl.ds(pl.multiple_of(half + ring_rows, CHUNK), direct_rows)
    g_send_buf[CHUNK:, :] = g_mine[direct, :].astype(F32)
    direct_across = remote(
        g_send_buf.at[pl.ds(CHUNK, direct_rows)], g_got.at[direct], g_send.at[1], g_recv.at[1], across
    )
    direct_across.start()

    def prepare(which, matrix):
        @pl.loop(0, norb // LANES)
        def _(i):
            block = pl.ds(pl.multiple_of(i * LANES, LANES), LANES)
            turned[which, :, block] = matrix[block, :].astype(F32).T.astype(BF16)

        own = pl.ds(pl.multiple_of(m * rows, CHUNK), rows)
        cols[which] = turned[which, own, :].astype(F32).T.astype(BF16)

    prepare(0, g_mine)

    occ_copy.wait_recv()
    own_one = off_ref[0] == 1
    own_occ = occ_mine[0:1, 0:1]
    other_occ = occ_got[0:1, 0:1]
    one_sel = jnp.where(own_one, 1.0, 0.0)
    is_one = (one_sel, 1.0 - one_sel)
    low2 = jnp.where(e >= 2, 1.0, 0.0)
    high2 = jnp.where(e < energies - 2, 1.0, 0.0)
    on_core = core.astype(F32)
    third = jnp.where((e > 0) & (e < energies - 1), 1.0, 0.0)
    weights = []
    for occ, one in zip((own_occ, other_occ), is_one):
        weights.append(
            (
                (occ + 1.0) * ((1.0 - one) * low2),
                occ * ((1.0 - one) * high2),
                (occ + on_core) * one,
                (occ + (1.0 - on_core)) * (one * third),
            )
        )

    own_to_sibling.wait_recv()

    def take_chunk(i):
        to_up(i).wait_recv()
        to_down(i).wait_recv()
        to_sibling(i).start()

    def couple(i, which):
        w = weights[which]
        combined = w[0] * near[0, at(i), :] + w[1] * near[1, at(i), :]
        combined = combined + (w[2] * near[2, at(i), :] + w[3] * near[3, at(i), :])
        coupled[which, at(i), :] = dot(combined.astype(BF16), turned[which]).astype(BF16)

    def ring_slice(step, base):
        behind = x_at - way * step + ALONG_X
        return rows_at(base + lax.rem(behind, ALONG_X) * CHUNK)

    def ring_copy(step):
        there = ring_slice(step, half)
        return remote(g_got.at[there], g_got.at[there], g_send.at[2 + step], g_recv.at[2 + step], ring_next)

    def ring_arrival(step):
        there = ring_slice(step, half)
        return remote(
            g_got.at[there], g_got.at[there], g_send.at[1 + step], g_recv.at[1 + step], ring_next
        )

    def share_slice(step, base):
        there = ring_slice(step, base)
        return remote(g_got.at[there], g_got.at[there], g_send.at[5 + step], g_recv.at[5 + step], sibling)

    def share_direct(base):
        there = pl.ds(pl.multiple_of(base + ring_rows, CHUNK), direct_rows)
        return remote(g_got.at[there], g_got.at[there], g_send.at[9], g_recv.at[9], sibling)

    def chunk_step(i):
        take_chunk(i)
        to_sibling(i).wait_recv()
        couple(i, 0)

    def chunk_steps(first, last):
        pl.loop(first, last)(chunk_step)

    chunk_steps(0, 1)
    slice_across.wait_recv()
    ring_copy(0).start()
    share_slice(0, half).start()
    chunk_steps(1, 3)
    ring_arrival(1).wait_recv()
    ring_copy(1).start()
    share_slice(1, half).start()
    chunk_steps(3, 4)
    ring_arrival(2).wait_recv()
    ring_copy(2).start()
    share_slice(2, half).start()
    direct_across.wait_recv()
    share_direct(half).start()
    chunk_steps(4, 5)
    ring_arrival(3).wait_recv()
    share_slice(3, half).start()
    theirs = (1 - core) * rows
    for step in range(ALONG_X):
        share_slice(step, theirs).wait_recv()
    share_direct(theirs).wait_recv()
    prepare(1, g_got)

    @pl.loop(0, 5)
    def _(i):
        couple(i, 1)

    @pl.loop(5, chunks)
    def _(i):
        chunk_step(i)
        couple(i, 1)

    def partial(j, base):
        there = pl.ds(pl.multiple_of(base, CHUNK), rows)
        return dot(cols[0, there, :], coupled[0, :, j]) + dot(cols[1, there, :], coupled[1, :, j])

    pieces = [slice(start, min(start + PIECE, norb)) for start in range(0, norb, PIECE)]
    for k, j in enumerate(pieces):
        p_out[:, j] = partial(j, (1 - m) * rows)
        to_partner(k, j).start()
    for j in pieces:
        o_ref[0, :, j] = partial(j, m * rows) * 0.5
    for k, j in enumerate(pieces):
        to_partner(k, j).wait_recv()
        o_ref[0, :, j] = o_ref[0, :, j] + p_in[:, j] * 0.5
    for k, j in enumerate(pieces):
        to_partner(k, j).wait_send()

    @pl.loop(0, chunks)
    def _(i):
        to_up(i).wait_send()
        to_down(i).wait_send()
        to_sibling(i).wait_send()

    own_to_sibling.wait_send()
    slice_across.wait_send()
    occ_copy.wait_send()
    direct_across.wait_send()
    for step in range(ALONG_X - 1):
        ring_copy(step).wait_send()
    for step in range(ALONG_X):
        share_slice(step, half).wait_send()
    share_direct(half).wait_send()


def shards(energies, spectral, coupling, offsets, occupation):
    _, rows, norb = spectral.shape
    chunks = rows // CHUNK
    dma = pltpu.SemaphoreType.DMA
    anywhere = pl.BlockSpec(memory_space=pltpu.HBM)
    scalar = pl.BlockSpec(memory_space=pltpu.SMEM)
    return pl.pallas_call(
        functools.partial(kernel, energies),
        out_shape=jax.ShapeDtypeStruct(spectral.shape, F32),
        in_specs=[anywhere, anywhere, scalar, scalar],
        out_specs=pl.BlockSpec(memory_space=pltpu.VMEM),
        scratch_shapes=[
            pltpu.VMEM((4, rows, norb), F32),
            pltpu.VMEM((norb, norb), BF16),
            pltpu.VMEM((rows - (ALONG_X - 1) * CHUNK, norb), F32),
            pltpu.VMEM((norb, norb), F32),
            pltpu.VMEM((2, norb, norb), BF16),
            pltpu.VMEM((2, norb, rows), BF16),
            pltpu.VMEM((2, rows, norb), BF16),
            pltpu.VMEM((rows, norb), F32),
            pltpu.VMEM((rows, norb), F32),
            pltpu.VMEM((8, 128), F32),
            pltpu.VMEM((8, 128), F32),
            dma,
            dma((2, chunks)),
            dma((2, chunks)),
            dma((chunks,)),
            dma((chunks,)),
            dma,
            dma,
            dma((10,)),
            dma((10,)),
            dma,
            dma,
            dma((-(-norb // PIECE),)),
            dma((-(-norb // PIECE),)),
        ],
        compiler_params=pltpu.CompilerParams(
            collective_id=0, has_side_effects=True, vmem_limit_bytes=48 << 20
        ),
        name="born_step",
    )(pltpu.with_memory_space_constraint(spectral, pltpu.HBM), pltpu.with_memory_space_constraint(coupling, pltpu.HBM), offsets, occupation)


def solution(mesh):
    return jax.shard_map(
        functools.partial(shards, mesh.shape["energy"]),
        mesh=mesh,
        in_specs=(P("energy", "mode", None), P("mode", None, None), P("mode"), P("mode", "energy")),
        out_specs=P("energy", "mode", None),
        check_vma=False,
    )
```

```python
import functools

import jax
import jax.numpy as jnp
from jax import lax
from jax.experimental import pallas as pl
from jax.experimental.pallas import tpu as pltpu
from jax.sharding import PartitionSpec as P

MESH = pl.DeviceIdType.MESH
CORES, ALONG_Z, ALONG_X = 2, 8, 4
CHUNK = 64
LANES = 128
PIECE = 256
EARLY = 5
AHEAD = 5
F32, BF16 = jnp.float32, jnp.bfloat16


def dot(a, b):
    return jnp.dot(a, b, preferred_element_type=F32)


def kernel(
    energies,
    x_ref,
    g_ref,
    off_ref,
    occ_ref,
    o_ref,
    near,
    g_mine,
    g_send_buf,
    g_got,
    turned,
    cols,
    coupled,
    p_out,
    p_in,
    occ_mine,
    occ_got,
    load_sem,
    near_send,
    near_recv,
    fwd_send,
    fwd_recv,
    sib_send,
    sib_recv,
    g_send,
    g_recv,
    occ_send,
    occ_recv,
    p_send,
    p_recv,
):
    e = lax.axis_index("energy")
    m = lax.axis_index("mode")
    rows, norb = x_ref.shape[1], x_ref.shape[2]
    chunks = rows // CHUNK
    core = e % CORES
    x_at = (e // (CORES * ALONG_Z)) % ALONG_X
    first = (lax.rem(e + energies - 2 + 4 * core, energies), m)
    second = (lax.rem(e + energies + 2 - 4 * core, energies), m)
    sibling = (e + 1 - 2 * core, m)
    partner = (e, 1 - m)
    across = (lax.rem(e + energies // 2, energies), 1 - m)
    z_at = (e // CORES) % ALONG_Z
    way = jnp.where(z_at < ALONG_Z // 2, -1, 1)
    x_next = lax.rem(x_at + way + ALONG_X, ALONG_X)
    x_last = lax.rem(x_at - way + ALONG_X, ALONG_X)
    ring_next = (e + (x_next - x_at) * (CORES * ALONG_Z), m)
    ring_last = (e + (x_last - x_at) * (CORES * ALONG_Z), m)

    load = pltpu.make_async_copy(g_ref.at[0], g_mine, load_sem)
    load.start()
    barrier = pltpu.get_barrier_semaphore()
    greeted = [first, second, sibling, partner, across, ring_next, ring_last]
    for device in greeted:
        pl.semaphore_signal(barrier, inc=1, device_id=device, device_id_type=MESH)
    pl.semaphore_wait(barrier, len(greeted))

    def remote(src, dst, send, recv, device):
        return pltpu.make_async_remote_copy(
            src_ref=src, dst_ref=dst, send_sem=send, recv_sem=recv, device_id=device, device_id_type=MESH
        )

    def at(i, base=0):
        return pl.ds(pl.multiple_of(base + i * CHUNK, CHUNK), CHUNK)

    def rows_at(start):
        return pl.ds(pl.multiple_of(start, CHUNK), CHUNK)

    def to_first(i):
        return remote(x_ref.at[0, at(i)], near.at[0, at(i)], near_send.at[0, i], near_recv.at[0, i], first)

    def to_second(i):
        return remote(x_ref.at[0, at(i)], near.at[1, at(i)], near_send.at[1, i], near_recv.at[1, i], second)

    def to_sibling(i):
        return remote(near.at[0, at(i)], near.at[3, at(i)], fwd_send.at[i], fwd_recv.at[i], sibling)

    def to_partner(k, j):
        return remote(p_out.at[:, j], p_in.at[:, j], p_send.at[k], p_recv.at[k], partner)

    own_to_sibling = remote(x_ref.at[0], near.at[2], sib_send, sib_recv, sibling)

    @pl.loop(0, chunks)
    def _(i):
        to_first(i).start()

    own_to_sibling.start()

    load.wait()
    half = core * rows
    mine = half + x_at * CHUNK
    g_send_buf[0:CHUNK, :] = g_mine[rows_at(mine), :].astype(F32)
    slice_across = remote(
        g_send_buf.at[pl.ds(0, CHUNK)], g_got.at[rows_at(mine)], g_send.at[0], g_recv.at[0], across
    )
    slice_across.start()
    occ_mine[...] = jnp.full(occ_mine.shape, occ_ref[0, 0].astype(F32), F32)
    occ_copy = remote(occ_mine, occ_got, occ_send, occ_recv, partner)
    occ_copy.start()
    ring_rows = ALONG_X * CHUNK
    direct_rows = rows - ring_rows
    direct = pl.ds(pl.multiple_of(half + ring_rows, CHUNK), direct_rows)
    g_send_buf[CHUNK:, :] = g_mine[direct, :].astype(F32)
    direct_across = remote(
        g_send_buf.at[pl.ds(CHUNK, direct_rows)], g_got.at[direct], g_send.at[1], g_recv.at[1], across
    )
    direct_across.start()

    def prepare(which, matrix):
        @pl.loop(0, norb // LANES)
        def _(i):
            block = pl.ds(pl.multiple_of(i * LANES, LANES), LANES)
            turned[which, :, block] = matrix[block, :].astype(F32).T.astype(BF16)

        own = pl.ds(pl.multiple_of(m * rows, CHUNK), rows)
        cols[which] = turned[which, own, :].astype(F32).T.astype(BF16)

    prepare(0, g_mine)

    occ_copy.wait_recv()
    own_occ = occ_mine[0:1, 0:1]
    other_occ = occ_got[0:1, 0:1]
    own_one = off_ref[0] == 1
    occ_one = jnp.where(own_one, own_occ, other_occ)
    occ_two = jnp.where(own_one, other_occ, own_occ)
    low2 = jnp.where(e >= 2, 1.0, 0.0)
    high2 = jnp.where(e < energies - 2, 1.0, 0.0)
    on_core = core.astype(F32)
    ends = jnp.where((e > 0) & (e < energies - 1), 1.0, 0.0)
    which_mode = (jnp.where(own_one, 0, 1), jnp.where(own_one, 1, 0))
    from_below = (occ_two + 1.0) * low2
    from_above = occ_two * high2
    weights = (
        jnp.where(core == 0, from_above, from_below),
        jnp.where(core == 0, from_below, from_above),
        occ_one + on_core,
        (occ_one + (1.0 - on_core)) * ends,
    )

    own_to_sibling.wait_recv()

    def combine(i, which):
        a, b = (2, 3) if which == 0 else (0, 1)
        return (weights[a] * near[a, at(i), :] + weights[b] * near[b, at(i), :]).astype(BF16)

    def couple(there, which, combined):
        coupled[which, there, :] = dot(combined, turned[which_mode[which]]).astype(BF16)

    def ring_slice(step, base):
        behind = x_at - way * step + ALONG_X
        return rows_at(base + lax.rem(behind, ALONG_X) * CHUNK)

    def ring_copy(step):
        there = ring_slice(step, half)
        return remote(g_got.at[there], g_got.at[there], g_send.at[2 + step], g_recv.at[2 + step], ring_next)

    def ring_arrival(step):
        there = ring_slice(step, half)
        return remote(
            g_got.at[there], g_got.at[there], g_send.at[1 + step], g_recv.at[1 + step], ring_next
        )

    def share_slice(step, base):
        there = ring_slice(step, base)
        return remote(g_got.at[there], g_got.at[there], g_send.at[5 + step], g_recv.at[5 + step], sibling)

    def share_direct(base):
        there = pl.ds(pl.multiple_of(base + ring_rows, CHUNK), direct_rows)
        return remote(g_got.at[there], g_got.at[there], g_send.at[9], g_recv.at[9], sibling)

    def first_steps(start, stop):
        @pl.loop(start, stop)
        def _(i):
            to_first(i).wait_recv()
            to_sibling(i).start()
            to_sibling(i).wait_recv()
            coupled[0, at(i), :] = combine(i, 0)

    def second_step(i):
        to_second(i).wait_recv()
        coupled[1, at(i), :] = combine(i, 1)

    def second_steps(start, stop):
        pl.loop(start, stop)(second_step)

    first_steps(0, 3)
    slice_across.wait_recv()
    ring_copy(0).start()
    share_slice(0, half).start()
    first_steps(3, 5)
    ring_arrival(1).wait_recv()
    ring_copy(1).start()
    share_slice(1, half).start()
    first_steps(5, AHEAD)

    @pl.loop(0, chunks)
    def _(i):
        to_second(i).start()

    first_steps(AHEAD, chunks)
    ring_arrival(2).wait_recv()
    ring_copy(2).start()
    share_slice(2, half).start()
    direct_across.wait_recv()
    share_direct(half).start()
    second_steps(0, 2)
    ring_arrival(3).wait_recv()
    share_slice(3, half).start()
    theirs = (1 - core) * rows
    for step in range(ALONG_X):
        share_slice(step, theirs).wait_recv()
    share_direct(theirs).wait_recv()
    prepare(1, g_got)
    couple(pl.ds(0, rows), 0, coupled[0])
    second_steps(2, EARLY)
    early = pl.ds(0, EARLY * CHUNK)
    couple(early, 1, coupled[1, early, :])
    for i in range(EARLY, chunks):
        to_second(i).wait_recv()
        couple(at(i), 1, combine(i, 1))

    def partial(j, base):
        there = pl.ds(pl.multiple_of(base, CHUNK), rows)
        return dot(cols[which_mode[0], there, :], coupled[0, :, j]) + dot(
            cols[which_mode[1], there, :], coupled[1, :, j]
        )

    edges = [0, *range(norb % PIECE, norb + 1, PIECE)]
    pieces = [slice(a, b) for a, b in zip(edges, edges[1:])]
    for k, j in enumerate(pieces):
        p_out[:, j] = partial(j, (1 - m) * rows)
        to_partner(k, j).start()
    for j in pieces:
        o_ref[0, :, j] = partial(j, m * rows) * 0.5
    for k, j in enumerate(pieces):
        to_partner(k, j).wait_recv()
        o_ref[0, :, j] = o_ref[0, :, j] + p_in[:, j] * 0.5
    for k, j in enumerate(pieces):
        to_partner(k, j).wait_send()

    @pl.loop(0, chunks)
    def _(i):
        to_first(i).wait_send()
        to_second(i).wait_send()
        to_sibling(i).wait_send()

    own_to_sibling.wait_send()
    slice_across.wait_send()
    occ_copy.wait_send()
    direct_across.wait_send()
    for step in range(ALONG_X - 1):
        ring_copy(step).wait_send()
    for step in range(ALONG_X):
        share_slice(step, half).wait_send()
    share_direct(half).wait_send()


def shards(energies, spectral, coupling, offsets, occupation):
    _, rows, norb = spectral.shape
    chunks = rows // CHUNK
    dma = pltpu.SemaphoreType.DMA
    scalar = pl.BlockSpec(memory_space=pltpu.SMEM)
    in_hbm = pl.BlockSpec(memory_space=pltpu.HBM)
    return pl.pallas_call(
        functools.partial(kernel, energies),
        out_shape=jax.ShapeDtypeStruct(spectral.shape, F32),
        in_specs=[in_hbm, in_hbm, scalar, scalar],
        out_specs=pl.BlockSpec(memory_space=pltpu.VMEM),
        scratch_shapes=[
            pltpu.VMEM((4, rows, norb), F32),
            pltpu.VMEM((norb, norb), BF16),
            pltpu.VMEM((rows - (ALONG_X - 1) * CHUNK, norb), F32),
            pltpu.VMEM((norb, norb), F32),
            pltpu.VMEM((2, norb, norb), BF16),
            pltpu.VMEM((2, norb, rows), BF16),
            pltpu.VMEM((2, rows, norb), BF16),
            pltpu.VMEM((rows, norb), F32),
            pltpu.VMEM((rows, norb), F32),
            pltpu.VMEM((8, 128), F32),
            pltpu.VMEM((8, 128), F32),
            dma,
            dma((2, chunks)),
            dma((2, chunks)),
            dma((chunks,)),
            dma((chunks,)),
            dma,
            dma,
            dma((10,)),
            dma((10,)),
            dma,
            dma,
            dma((-(-norb // PIECE),)),
            dma((-(-norb // PIECE),)),
        ],
        compiler_params=pltpu.CompilerParams(
            collective_id=0, has_side_effects=True, vmem_limit_bytes=48 << 20
        ),
        name="born_step",
    )(*(pltpu.with_memory_space_constraint(a, pltpu.HBM) for a in (spectral, coupling)), offsets, occupation)


def solution(mesh):
    return jax.shard_map(
        functools.partial(shards, mesh.shape["energy"]),
        mesh=mesh,
        in_specs=(P("energy", "mode", None), P("mode", None, None), P("mode"), P("mode", "energy")),
        out_specs=P("energy", "mode", None),
        check_vma=False,
    )
```

```python
import functools

import jax
import jax.numpy as jnp
from jax import lax
from jax.experimental import pallas as pl
from jax.experimental.pallas import tpu as pltpu
from jax.sharding import PartitionSpec as P

MESH = pl.DeviceIdType.MESH
CORES, ALONG_Z, ALONG_X = 2, 8, 4
CHUNK = 64
LANES = 128
PIECE = 256
EARLY = 5
SENT = 4
F32, BF16 = jnp.float32, jnp.bfloat16


def dot(a, b):
    return jnp.dot(a, b, preferred_element_type=F32)


def kernel(
    energies,
    x_ref,
    g_ref,
    off_ref,
    occ_ref,
    o_ref,
    near,
    g_mine,
    g_send_buf,
    g_got,
    turned,
    cols,
    coupled,
    p_out,
    p_in,
    occ_mine,
    occ_got,
    load_sem,
    near_send,
    near_recv,
    fwd_send,
    fwd_recv,
    sib_send,
    sib_recv,
    g_send,
    g_recv,
    occ_send,
    occ_recv,
    p_send,
    p_recv,
):
    e = lax.axis_index("energy")
    m = lax.axis_index("mode")
    rows, norb = x_ref.shape[1], x_ref.shape[2]
    chunks = rows // CHUNK
    core = e % CORES
    x_at = (e // (CORES * ALONG_Z)) % ALONG_X
    first = (lax.rem(e + energies - 2 + 4 * core, energies), m)
    second = (lax.rem(e + energies + 2 - 4 * core, energies), m)
    sibling = (e + 1 - 2 * core, m)
    partner = (e, 1 - m)
    across = (lax.rem(e + energies // 2, energies), 1 - m)
    z_at = (e // CORES) % ALONG_Z
    way = jnp.where(z_at < ALONG_Z // 2, -1, 1)
    x_next = lax.rem(x_at + way + ALONG_X, ALONG_X)
    x_last = lax.rem(x_at - way + ALONG_X, ALONG_X)
    ring_next = (e + (x_next - x_at) * (CORES * ALONG_Z), m)
    ring_last = (e + (x_last - x_at) * (CORES * ALONG_Z), m)

    load = pltpu.make_async_copy(g_ref.at[0], g_mine, load_sem)
    load.start()
    barrier = pltpu.get_barrier_semaphore()
    greeted = [first, second, sibling, partner, across, ring_next, ring_last]
    for device in greeted:
        pl.semaphore_signal(barrier, inc=1, device_id=device, device_id_type=MESH)
    pl.semaphore_wait(barrier, len(greeted))

    def remote(src, dst, send, recv, device):
        return pltpu.make_async_remote_copy(
            src_ref=src, dst_ref=dst, send_sem=send, recv_sem=recv, device_id=device, device_id_type=MESH
        )

    def at(i, base=0):
        return pl.ds(pl.multiple_of(base + i * CHUNK, CHUNK), CHUNK)

    def rows_at(start):
        return pl.ds(pl.multiple_of(start, CHUNK), CHUNK)

    def to_first(i):
        return remote(x_ref.at[0, at(i)], near.at[0, at(i)], near_send.at[0, i], near_recv.at[0, i], first)

    def to_second(i):
        return remote(x_ref.at[0, at(i)], near.at[1, at(i)], near_send.at[1, i], near_recv.at[1, i], second)

    def to_sibling(i):
        return remote(near.at[0, at(i)], near.at[3, at(i)], fwd_send.at[i], fwd_recv.at[i], sibling)

    def to_partner(k, j):
        return remote(p_out.at[:, j], p_in.at[:, j], p_send.at[k], p_recv.at[k], partner)

    own_to_sibling = remote(x_ref.at[0], near.at[2], sib_send, sib_recv, sibling)

    @pl.loop(0, chunks)
    def _(i):
        to_first(i).start()

    own_to_sibling.start()

    load.wait()
    half = core * rows
    mine = half + x_at * CHUNK
    g_send_buf[0:CHUNK, :] = g_mine[rows_at(mine), :].astype(F32)
    slice_across = remote(
        g_send_buf.at[pl.ds(0, CHUNK)], g_got.at[rows_at(mine)], g_send.at[0], g_recv.at[0], across
    )
    slice_across.start()
    occ_mine[...] = jnp.full(occ_mine.shape, occ_ref[0, 0].astype(F32), F32)
    occ_copy = remote(occ_mine, occ_got, occ_send, occ_recv, partner)
    occ_copy.start()
    ring_rows = ALONG_X * CHUNK
    direct_rows = rows - ring_rows
    direct = pl.ds(pl.multiple_of(half + ring_rows, CHUNK), direct_rows)
    g_send_buf[CHUNK:, :] = g_mine[direct, :].astype(F32)
    direct_across = remote(
        g_send_buf.at[pl.ds(CHUNK, direct_rows)], g_got.at[direct], g_send.at[1], g_recv.at[1], across
    )
    direct_across.start()

    def prepare(which, matrix):
        @pl.loop(0, norb // LANES)
        def _(i):
            block = pl.ds(pl.multiple_of(i * LANES, LANES), LANES)
            turned[which, :, block] = matrix[block, :].astype(F32).T.astype(BF16)

        own = pl.ds(pl.multiple_of(m * rows, CHUNK), rows)
        cols[which] = turned[which, own, :].astype(F32).T.astype(BF16)

    prepare(0, g_mine)

    occ_copy.wait_recv()
    own_occ = occ_mine[0:1, 0:1]
    other_occ = occ_got[0:1, 0:1]
    own_one = off_ref[0] == 1
    occ_one = jnp.where(own_one, own_occ, other_occ)
    occ_two = jnp.where(own_one, other_occ, own_occ)
    low2 = jnp.where(e >= 2, 1.0, 0.0)
    high2 = jnp.where(e < energies - 2, 1.0, 0.0)
    on_core = core.astype(F32)
    ends = jnp.where((e > 0) & (e < energies - 1), 1.0, 0.0)
    which_mode = (jnp.where(own_one, 0, 1), jnp.where(own_one, 1, 0))
    from_below = (occ_two + 1.0) * low2
    from_above = occ_two * high2
    weights = (
        jnp.where(core == 0, from_above, from_below),
        jnp.where(core == 0, from_below, from_above),
        occ_one + on_core,
        (occ_one + (1.0 - on_core)) * ends,
    )

    own_to_sibling.wait_recv()

    def combine(i, which):
        a, b = (2, 3) if which == 0 else (0, 1)
        return (weights[a] * near[a, at(i), :] + weights[b] * near[b, at(i), :]).astype(BF16)

    def couple(there, which, combined):
        coupled[which, there, :] = dot(combined, turned[which_mode[which]]).astype(BF16)

    def ring_slice(step, base):
        behind = x_at - way * step + ALONG_X
        return rows_at(base + lax.rem(behind, ALONG_X) * CHUNK)

    def ring_copy(step):
        there = ring_slice(step, half)
        return remote(g_got.at[there], g_got.at[there], g_send.at[2 + step], g_recv.at[2 + step], ring_next)

    def ring_arrival(step):
        there = ring_slice(step, half)
        return remote(
            g_got.at[there], g_got.at[there], g_send.at[1 + step], g_recv.at[1 + step], ring_next
        )

    def share_slice(step, base):
        there = ring_slice(step, base)
        return remote(g_got.at[there], g_got.at[there], g_send.at[5 + step], g_recv.at[5 + step], sibling)

    def share_direct(base):
        there = pl.ds(pl.multiple_of(base + ring_rows, CHUNK), direct_rows)
        return remote(g_got.at[there], g_got.at[there], g_send.at[9], g_recv.at[9], sibling)

    def first_steps(start, stop):
        @pl.loop(start, stop)
        def _(i):
            to_first(i).wait_recv()
            to_sibling(i).start()
            to_sibling(i).wait_recv()
            coupled[0, at(i), :] = combine(i, 0)

    def second_step(i):
        to_second(i).wait_recv()
        coupled[1, at(i), :] = combine(i, 1)

    def second_steps(start, stop):
        pl.loop(start, stop)(second_step)

    slice_across.wait_recv()
    ring_copy(0).start()
    share_slice(0, half).start()
    first_steps(0, 3)
    to_first(SENT).wait_send()

    @pl.loop(0, chunks)
    def _(i):
        to_second(i).start()

    ring_arrival(1).wait_recv()
    ring_copy(1).start()
    share_slice(1, half).start()
    first_steps(3, 5)
    ring_arrival(2).wait_recv()
    ring_copy(2).start()
    share_slice(2, half).start()
    first_steps(5, chunks)
    direct_across.wait_recv()
    share_direct(half).start()
    ring_arrival(3).wait_recv()
    share_slice(3, half).start()
    second_steps(0, 2)
    theirs = (1 - core) * rows
    for step in range(ALONG_X):
        share_slice(step, theirs).wait_recv()
    share_direct(theirs).wait_recv()
    prepare(1, g_got)
    couple(pl.ds(0, rows), 0, coupled[0])
    second_steps(2, EARLY)
    early = pl.ds(0, EARLY * CHUNK)
    couple(early, 1, coupled[1, early, :])
    for i in range(EARLY, chunks):
        to_second(i).wait_recv()
        couple(at(i), 1, combine(i, 1))

    def partial(j, base):
        there = pl.ds(pl.multiple_of(base, CHUNK), rows)
        return dot(cols[which_mode[0], there, :], coupled[0, :, j]) + dot(
            cols[which_mode[1], there, :], coupled[1, :, j]
        )

    edges = [0, *range(norb % PIECE, norb + 1, PIECE)]
    pieces = [slice(a, b) for a, b in zip(edges, edges[1:])]
    for k, j in enumerate(pieces):
        p_out[:, j] = partial(j, (1 - m) * rows)
        to_partner(k, j).start()
    for j in pieces:
        o_ref[0, :, j] = partial(j, m * rows) * 0.5
    for k, j in enumerate(pieces):
        to_partner(k, j).wait_recv()
        o_ref[0, :, j] = o_ref[0, :, j] + p_in[:, j] * 0.5
    for k, j in enumerate(pieces):
        to_partner(k, j).wait_send()

    @pl.loop(0, chunks)
    def _(i):
        to_second(i).wait_send()
        to_sibling(i).wait_send()

    for i in range(chunks):
        if i != SENT:
            to_first(i).wait_send()
    own_to_sibling.wait_send()
    slice_across.wait_send()
    occ_copy.wait_send()
    direct_across.wait_send()
    for step in range(ALONG_X - 1):
        ring_copy(step).wait_send()
    for step in range(ALONG_X):
        share_slice(step, half).wait_send()
    share_direct(half).wait_send()


def shards(energies, spectral, coupling, offsets, occupation):
    _, rows, norb = spectral.shape
    chunks = rows // CHUNK
    dma = pltpu.SemaphoreType.DMA
    scalar = pl.BlockSpec(memory_space=pltpu.SMEM)
    in_hbm = pl.BlockSpec(memory_space=pltpu.HBM)
    return pl.pallas_call(
        functools.partial(kernel, energies),
        out_shape=jax.ShapeDtypeStruct(spectral.shape, F32),
        in_specs=[in_hbm, in_hbm, scalar, scalar],
        out_specs=pl.BlockSpec(memory_space=pltpu.VMEM),
        scratch_shapes=[
            pltpu.VMEM((4, rows, norb), F32),
            pltpu.VMEM((norb, norb), BF16),
            pltpu.VMEM((rows - (ALONG_X - 1) * CHUNK, norb), F32),
            pltpu.VMEM((norb, norb), F32),
            pltpu.VMEM((2, norb, norb), BF16),
            pltpu.VMEM((2, norb, rows), BF16),
            pltpu.VMEM((2, rows, norb), BF16),
            pltpu.VMEM((rows, norb), F32),
            pltpu.VMEM((rows, norb), F32),
            pltpu.VMEM((8, 128), F32),
            pltpu.VMEM((8, 128), F32),
            dma,
            dma((2, chunks)),
            dma((2, chunks)),
            dma((chunks,)),
            dma((chunks,)),
            dma,
            dma,
            dma((10,)),
            dma((10,)),
            dma,
            dma,
            dma((-(-norb // PIECE),)),
            dma((-(-norb // PIECE),)),
        ],
        compiler_params=pltpu.CompilerParams(
            collective_id=0, has_side_effects=True, vmem_limit_bytes=48 << 20
        ),
        name="born_step",
    )(*(pltpu.with_memory_space_constraint(a, pltpu.HBM) for a in (spectral, coupling)), offsets, occupation)


def solution(mesh):
    return jax.shard_map(
        functools.partial(shards, mesh.shape["energy"]),
        mesh=mesh,
        in_specs=(P("energy", "mode", None), P("mode", None, None), P("mode"), P("mode", "energy")),
        out_specs=P("energy", "mode", None),
        check_vma=False,
    )
```

```python
import functools

import jax
import jax.numpy as jnp
from jax import lax
from jax.experimental import pallas as pl
from jax.experimental.pallas import tpu as pltpu
from jax.sharding import PartitionSpec as P

MESH = pl.DeviceIdType.MESH
CORES, ALONG_Z, ALONG_X = 2, 8, 4
CHUNK = 64
LANES = 128
PIECE = 256
EARLY = 5
SENT = 4
F32, BF16 = jnp.float32, jnp.bfloat16


def dot(a, b):
    return jnp.dot(a, b, preferred_element_type=F32)


def kernel(
    energies,
    x_ref,
    g_ref,
    off_ref,
    occ_ref,
    o_ref,
    near,
    g_mine,
    g_send_buf,
    g_got,
    turned,
    cols,
    coupled,
    p_out,
    p_in,
    occ_mine,
    occ_got,
    load_sem,
    near_send,
    near_recv,
    fwd_send,
    fwd_recv,
    sib_send,
    sib_recv,
    g_send,
    g_recv,
    occ_send,
    occ_recv,
    p_send,
    p_recv,
):
    e = lax.axis_index("energy")
    m = lax.axis_index("mode")
    rows, norb = x_ref.shape[1], x_ref.shape[2]
    chunks = rows // CHUNK
    core = e % CORES
    x_at = (e // (CORES * ALONG_Z)) % ALONG_X
    first = (lax.rem(e + energies - 2 + 4 * core, energies), m)
    second = (lax.rem(e + energies + 2 - 4 * core, energies), m)
    sibling = (e + 1 - 2 * core, m)
    partner = (e, 1 - m)
    across = (lax.rem(e + energies // 2, energies), 1 - m)
    z_at = (e // CORES) % ALONG_Z
    way = jnp.where(z_at < ALONG_Z // 2, -1, 1)
    x_next = lax.rem(x_at + way + ALONG_X, ALONG_X)
    x_last = lax.rem(x_at - way + ALONG_X, ALONG_X)
    ring_next = (e + (x_next - x_at) * (CORES * ALONG_Z), m)
    ring_last = (e + (x_last - x_at) * (CORES * ALONG_Z), m)

    load = pltpu.make_async_copy(g_ref.at[0], g_mine, load_sem)
    load.start()
    barrier = pltpu.get_barrier_semaphore()
    greeted = [first, second, sibling, partner, across, ring_last]
    for device in greeted:
        pl.semaphore_signal(barrier, inc=1, device_id=device, device_id_type=MESH)
    pl.semaphore_wait(barrier, len(greeted))

    def remote(src, dst, send, recv, device):
        return pltpu.make_async_remote_copy(
            src_ref=src, dst_ref=dst, send_sem=send, recv_sem=recv, device_id=device, device_id_type=MESH
        )

    def at(i, base=0):
        return pl.ds(pl.multiple_of(base + i * CHUNK, CHUNK), CHUNK)

    def rows_at(start):
        return pl.ds(pl.multiple_of(start, CHUNK), CHUNK)

    def to_first(i):
        return remote(x_ref.at[0, at(i)], near.at[0, at(i)], near_send.at[0, i], near_recv.at[0, i], first)

    def to_second(i):
        return remote(x_ref.at[0, at(i)], near.at[1, at(i)], near_send.at[1, i], near_recv.at[1, i], second)

    def to_sibling(i):
        return remote(near.at[0, at(i)], near.at[3, at(i)], fwd_send.at[i], fwd_recv.at[i], sibling)

    def to_partner(k, j):
        return remote(p_out.at[:, j], p_in.at[:, j], p_send.at[k], p_recv.at[k], partner)

    own_to_sibling = remote(x_ref.at[0], near.at[2], sib_send, sib_recv, sibling)

    @pl.loop(0, chunks)
    def _(i):
        to_first(i).start()

    own_to_sibling.start()

    load.wait()
    half = core * rows
    mine = half + x_at * CHUNK
    g_send_buf[0:CHUNK, :] = g_mine[rows_at(mine), :].astype(F32)
    slice_across = remote(
        g_send_buf.at[pl.ds(0, CHUNK)], g_got.at[rows_at(mine)], g_send.at[0], g_recv.at[0], across
    )
    slice_across.start()
    occ_mine[...] = jnp.full(occ_mine.shape, occ_ref[0, 0].astype(F32), F32)
    occ_copy = remote(occ_mine, occ_got, occ_send, occ_recv, partner)
    occ_copy.start()
    ring_rows = ALONG_X * CHUNK
    direct_rows = rows - ring_rows
    direct = pl.ds(pl.multiple_of(half + ring_rows, CHUNK), direct_rows)
    g_send_buf[CHUNK:, :] = g_mine[direct, :].astype(F32)
    direct_across = remote(
        g_send_buf.at[pl.ds(CHUNK, direct_rows)], g_got.at[direct], g_send.at[1], g_recv.at[1], across
    )
    direct_across.start()

    def prepare(which, matrix):
        @pl.loop(0, norb // LANES)
        def _(i):
            block = pl.ds(pl.multiple_of(i * LANES, LANES), LANES)
            turned[which, :, block] = matrix[block, :].astype(F32).T.astype(BF16)

        own = pl.ds(pl.multiple_of(m * rows, CHUNK), rows)
        cols[which] = turned[which, own, :].astype(F32).T.astype(BF16)

    prepare(0, g_mine)

    occ_copy.wait_recv()
    own_occ = occ_mine[0:1, 0:1]
    other_occ = occ_got[0:1, 0:1]
    own_one = off_ref[0] == 1
    occ_one = jnp.where(own_one, own_occ, other_occ)
    occ_two = jnp.where(own_one, other_occ, own_occ)
    low2 = jnp.where(e >= 2, 1.0, 0.0)
    high2 = jnp.where(e < energies - 2, 1.0, 0.0)
    on_core = core.astype(F32)
    ends = jnp.where((e > 0) & (e < energies - 1), 1.0, 0.0)
    which_mode = (jnp.where(own_one, 0, 1), jnp.where(own_one, 1, 0))
    from_below = (occ_two + 1.0) * low2
    from_above = occ_two * high2
    weights = (
        jnp.where(core == 0, from_above, from_below),
        jnp.where(core == 0, from_below, from_above),
        occ_one + on_core,
        (occ_one + (1.0 - on_core)) * ends,
    )

    own_to_sibling.wait_recv()

    def combine(i, which):
        a, b = (2, 3) if which == 0 else (0, 1)
        return (weights[a] * near[a, at(i), :] + weights[b] * near[b, at(i), :]).astype(BF16)

    def couple(there, which, combined):
        coupled[which, there, :] = dot(combined, turned[which_mode[which]]).astype(BF16)

    def ring_slice(step, base):
        behind = x_at - way * step + ALONG_X
        return rows_at(base + lax.rem(behind, ALONG_X) * CHUNK)

    def ring_copy(step):
        there = ring_slice(step, half)
        return remote(g_got.at[there], g_got.at[there], g_send.at[2 + step], g_recv.at[2 + step], ring_next)

    def ring_arrival(step):
        there = ring_slice(step, half)
        return remote(
            g_got.at[there], g_got.at[there], g_send.at[1 + step], g_recv.at[1 + step], ring_next
        )

    def share_slice(step, base):
        there = ring_slice(step, base)
        return remote(g_got.at[there], g_got.at[there], g_send.at[5 + step], g_recv.at[5 + step], sibling)

    def share_direct(base):
        there = pl.ds(pl.multiple_of(base + ring_rows, CHUNK), direct_rows)
        return remote(g_got.at[there], g_got.at[there], g_send.at[9], g_recv.at[9], sibling)

    def first_steps(start, stop):
        @pl.loop(start, stop)
        def _(i):
            to_first(i).wait_recv()
            to_sibling(i).start()
            to_sibling(i).wait_recv()
            coupled[0, at(i), :] = combine(i, 0)

    def second_step(i):
        to_second(i).wait_recv()
        coupled[1, at(i), :] = combine(i, 1)

    def second_steps(start, stop):
        pl.loop(start, stop)(second_step)

    slice_across.wait_recv()
    ring_copy(0).start()
    share_slice(0, half).start()
    first_steps(0, 3)
    to_first(SENT).wait_send()

    @pl.loop(0, chunks)
    def _(i):
        to_second(i).start()

    ring_arrival(1).wait_recv()
    ring_copy(1).start()
    share_slice(1, half).start()
    first_steps(3, 5)
    ring_arrival(2).wait_recv()
    ring_copy(2).start()
    share_slice(2, half).start()
    first_steps(5, chunks)
    direct_across.wait_recv()
    share_direct(half).start()
    ring_arrival(3).wait_recv()
    share_slice(3, half).start()
    second_steps(0, 2)
    theirs = (1 - core) * rows
    for step in range(ALONG_X):
        share_slice(step, theirs).wait_recv()
    share_direct(theirs).wait_recv()
    prepare(1, g_got)
    couple(pl.ds(0, rows), 0, coupled[0])
    second_steps(2, EARLY)
    early = pl.ds(0, EARLY * CHUNK)
    couple(early, 1, coupled[1, early, :])
    for i in range(EARLY, chunks - 1):
        to_second(i).wait_recv()
        couple(at(i), 1, combine(i, 1))
    last = at(chunks - 1)
    to_second(chunks - 1).wait_recv()
    combined = combine(chunks - 1, 1)

    def partial(j, base):
        there = pl.ds(pl.multiple_of(base, CHUNK), rows)
        return dot(cols[which_mode[0], there, :], coupled[0, :, j]) + dot(
            cols[which_mode[1], there, :], coupled[1, :, j]
        )

    edges = [0, 128, 384, 640, 768, 896]
    pieces = [slice(a, b) for a, b in zip(edges, edges[1:])]
    for k, j in enumerate(pieces):
        coupled[1, last, j] = dot(combined, turned[which_mode[1], :, j]).astype(BF16)
        p_out[:, j] = partial(j, (1 - m) * rows)
        to_partner(k, j).start()
    for j in pieces:
        o_ref[0, :, j] = partial(j, m * rows) * 0.5
    for k, j in enumerate(pieces):
        to_partner(k, j).wait_recv()
        o_ref[0, :, j] = o_ref[0, :, j] + p_in[:, j] * 0.5
    for k, j in enumerate(pieces):
        to_partner(k, j).wait_send()

    @pl.loop(0, chunks)
    def _(i):
        to_second(i).wait_send()
        to_sibling(i).wait_send()

    for i in range(chunks):
        if i != SENT:
            to_first(i).wait_send()
    own_to_sibling.wait_send()
    slice_across.wait_send()
    occ_copy.wait_send()
    direct_across.wait_send()
    for step in range(ALONG_X - 1):
        ring_copy(step).wait_send()
    for step in range(ALONG_X):
        share_slice(step, half).wait_send()
    share_direct(half).wait_send()


def shards(energies, spectral, coupling, offsets, occupation):
    _, rows, norb = spectral.shape
    chunks = rows // CHUNK
    dma = pltpu.SemaphoreType.DMA
    scalar = pl.BlockSpec(memory_space=pltpu.SMEM)
    in_hbm = pl.BlockSpec(memory_space=pltpu.HBM)
    return pl.pallas_call(
        functools.partial(kernel, energies),
        out_shape=jax.ShapeDtypeStruct(spectral.shape, F32),
        in_specs=[in_hbm, in_hbm, scalar, scalar],
        out_specs=pl.BlockSpec(memory_space=pltpu.VMEM),
        scratch_shapes=[
            pltpu.VMEM((4, rows, norb), F32),
            pltpu.VMEM((norb, norb), BF16),
            pltpu.VMEM((rows - (ALONG_X - 1) * CHUNK, norb), F32),
            pltpu.VMEM((norb, norb), F32),
            pltpu.VMEM((2, norb, norb), BF16),
            pltpu.VMEM((2, norb, rows), BF16),
            pltpu.VMEM((2, rows, norb), BF16),
            pltpu.VMEM((rows, norb), F32),
            pltpu.VMEM((rows, norb), F32),
            pltpu.VMEM((8, 128), F32),
            pltpu.VMEM((8, 128), F32),
            dma,
            dma((2, chunks)),
            dma((2, chunks)),
            dma((chunks,)),
            dma((chunks,)),
            dma,
            dma,
            dma((10,)),
            dma((10,)),
            dma,
            dma,
            dma((5,)),
            dma((5,)),
        ],
        compiler_params=pltpu.CompilerParams(
            collective_id=0, has_side_effects=True, vmem_limit_bytes=48 << 20
        ),
        name="born_step",
    )(*(pltpu.with_memory_space_constraint(a, pltpu.HBM) for a in (spectral, coupling)), offsets, occupation)


def solution(mesh):
    return jax.shard_map(
        functools.partial(shards, mesh.shape["energy"]),
        mesh=mesh,
        in_specs=(P("energy", "mode", None), P("mode", None, None), P("mode"), P("mode", "energy")),
        out_specs=P("energy", "mode", None),
        check_vma=False,
    )
```

```python
import functools

import jax
import jax.numpy as jnp
from jax import lax
from jax.experimental import pallas as pl
from jax.experimental.pallas import tpu as pltpu
from jax.sharding import PartitionSpec as P

MESH = pl.DeviceIdType.MESH
CORES, ALONG_Z, ALONG_X = 2, 8, 4
CHUNK = 64
LANES = 128
PIECE = 256
EARLY = 5
SENT = 4
F32, BF16 = jnp.float32, jnp.bfloat16


def dot(a, b):
    return jnp.dot(a, b, preferred_element_type=F32)


def kernel(
    energies,
    x_ref,
    g_ref,
    off_ref,
    occ_ref,
    o_ref,
    near,
    g_mine,
    g_send_buf,
    g_got,
    turned,
    cols,
    coupled,
    p_out,
    p_in,
    occ_mine,
    occ_got,
    load_sem,
    near_send,
    near_recv,
    fwd_send,
    fwd_recv,
    sib_send,
    sib_recv,
    g_send,
    g_recv,
    occ_send,
    occ_recv,
    p_send,
    p_recv,
):
    e = lax.axis_index("energy")
    m = lax.axis_index("mode")
    rows, norb = x_ref.shape[1], x_ref.shape[2]
    chunks = rows // CHUNK
    core = e % CORES
    x_at = (e // (CORES * ALONG_Z)) % ALONG_X
    first = (lax.rem(e + energies - 2 + 4 * core, energies), m)
    second = (lax.rem(e + energies + 2 - 4 * core, energies), m)
    sibling = (e + 1 - 2 * core, m)
    partner = (e, 1 - m)
    across = (lax.rem(e + energies // 2, energies), 1 - m)
    z_at = (e // CORES) % ALONG_Z
    way = jnp.where(z_at < ALONG_Z // 2, -1, 1)
    x_next = lax.rem(x_at + way + ALONG_X, ALONG_X)
    x_last = lax.rem(x_at - way + ALONG_X, ALONG_X)
    ring_next = (e + (x_next - x_at) * (CORES * ALONG_Z), m)
    ring_last = (e + (x_last - x_at) * (CORES * ALONG_Z), m)

    load = pltpu.make_async_copy(g_ref.at[0], g_mine, load_sem)
    load.start()
    barrier = pltpu.get_barrier_semaphore()
    greeted = [first, second, sibling, partner, across, ring_last]
    for device in greeted:
        pl.semaphore_signal(barrier, inc=1, device_id=device, device_id_type=MESH)
    pl.semaphore_wait(barrier, len(greeted))

    def remote(src, dst, send, recv, device):
        return pltpu.make_async_remote_copy(
            src_ref=src, dst_ref=dst, send_sem=send, recv_sem=recv, device_id=device, device_id_type=MESH
        )

    def at(i, base=0):
        return pl.ds(pl.multiple_of(base + i * CHUNK, CHUNK), CHUNK)

    def rows_at(start):
        return pl.ds(pl.multiple_of(start, CHUNK), CHUNK)

    def to_first(i):
        return remote(x_ref.at[0, at(i)], near.at[0, at(i)], near_send.at[0, i], near_recv.at[0, i], first)

    def to_second(i):
        return remote(x_ref.at[0, at(i)], near.at[1, at(i)], near_send.at[1, i], near_recv.at[1, i], second)

    def to_sibling(i):
        return remote(near.at[0, at(i)], near.at[3, at(i)], fwd_send.at[i], fwd_recv.at[i], sibling)

    def to_partner(k, j):
        return remote(p_out.at[:, j], p_in.at[:, j], p_send.at[k], p_recv.at[k], partner)

    own_to_sibling = remote(x_ref.at[0], near.at[2], sib_send, sib_recv, sibling)

    @pl.loop(0, chunks)
    def _(i):
        to_first(i).start()

    own_to_sibling.start()

    load.wait()
    half = core * rows
    mine = half + x_at * CHUNK
    g_send_buf[0:CHUNK, :] = g_mine[rows_at(mine), :].astype(F32)
    slice_across = remote(
        g_send_buf.at[pl.ds(0, CHUNK)], g_got.at[rows_at(mine)], g_send.at[0], g_recv.at[0], across
    )
    slice_across.start()
    occ_mine[...] = jnp.full(occ_mine.shape, occ_ref[0, 0].astype(F32), F32)
    occ_copy = remote(occ_mine, occ_got, occ_send, occ_recv, partner)
    occ_copy.start()
    ring_rows = ALONG_X * CHUNK
    direct_rows = rows - ring_rows
    direct = pl.ds(pl.multiple_of(half + ring_rows, CHUNK), direct_rows)
    g_send_buf[CHUNK:, :] = g_mine[direct, :].astype(F32)
    direct_across = remote(
        g_send_buf.at[pl.ds(CHUNK, direct_rows)], g_got.at[direct], g_send.at[1], g_recv.at[1], across
    )
    direct_across.start()

    def prepare(which, matrix):
        @pl.loop(0, norb // LANES)
        def _(i):
            block = pl.ds(pl.multiple_of(i * LANES, LANES), LANES)
            turned[which, :, block] = matrix[block, :].astype(F32).T.astype(BF16)

        own = pl.ds(pl.multiple_of(m * rows, CHUNK), rows)
        cols[which] = turned[which, own, :].astype(F32).T.astype(BF16)

    prepare(0, g_mine)

    occ_copy.wait_recv()
    own_occ = occ_mine[0:1, 0:1]
    other_occ = occ_got[0:1, 0:1]
    own_one = off_ref[0] == 1
    occ_one = jnp.where(own_one, own_occ, other_occ)
    occ_two = jnp.where(own_one, other_occ, own_occ)
    low2 = jnp.where(e >= 2, 1.0, 0.0)
    high2 = jnp.where(e < energies - 2, 1.0, 0.0)
    on_core = core.astype(F32)
    ends = jnp.where((e > 0) & (e < energies - 1), 1.0, 0.0)
    which_mode = (jnp.where(own_one, 0, 1), jnp.where(own_one, 1, 0))
    from_below = (occ_two + 1.0) * low2
    from_above = occ_two * high2
    weights = (
        jnp.where(core == 0, from_above, from_below),
        jnp.where(core == 0, from_below, from_above),
        occ_one + on_core,
        (occ_one + (1.0 - on_core)) * ends,
    )

    own_to_sibling.wait_recv()

    def combine(i, which):
        a, b = (2, 3) if which == 0 else (0, 1)
        return (weights[a] * near[a, at(i), :] + weights[b] * near[b, at(i), :]).astype(BF16)

    def couple(there, which, combined):
        coupled[which, there, :] = dot(combined, turned[which_mode[which]]).astype(BF16)

    def ring_slice(step, base):
        behind = x_at - way * step + ALONG_X
        return rows_at(base + lax.rem(behind, ALONG_X) * CHUNK)

    def ring_copy(step):
        there = ring_slice(step, half)
        return remote(g_got.at[there], g_got.at[there], g_send.at[2 + step], g_recv.at[2 + step], ring_next)

    def ring_arrival(step):
        there = ring_slice(step, half)
        return remote(
            g_got.at[there], g_got.at[there], g_send.at[1 + step], g_recv.at[1 + step], ring_next
        )

    def share_slice(step, base):
        there = ring_slice(step, base)
        return remote(g_got.at[there], g_got.at[there], g_send.at[5 + step], g_recv.at[5 + step], sibling)

    def share_direct(base):
        there = pl.ds(pl.multiple_of(base + ring_rows, CHUNK), direct_rows)
        return remote(g_got.at[there], g_got.at[there], g_send.at[9], g_recv.at[9], sibling)

    def first_steps(start, stop):
        @pl.loop(start, stop)
        def _(i):
            to_first(i).wait_recv()
            to_sibling(i).start()
            to_sibling(i).wait_recv()
            coupled[0, at(i), :] = combine(i, 0)

    def second_step(i):
        to_second(i).wait_recv()
        coupled[1, at(i), :] = combine(i, 1)

    def second_steps(start, stop):
        pl.loop(start, stop)(second_step)

    slice_across.wait_recv()
    ring_copy(0).start()
    share_slice(0, half).start()
    first_steps(0, 3)
    to_first(SENT).wait_send()

    @pl.loop(0, chunks)
    def _(i):
        to_second(i).start()

    ring_arrival(1).wait_recv()
    ring_copy(1).start()
    share_slice(1, half).start()
    first_steps(3, 5)
    ring_arrival(2).wait_recv()
    ring_copy(2).start()
    share_slice(2, half).start()
    first_steps(5, chunks)
    direct_across.wait_recv()
    share_direct(half).start()
    ring_arrival(3).wait_recv()
    share_slice(3, half).start()
    second_steps(0, 2)
    theirs = (1 - core) * rows
    for step in range(ALONG_X):
        share_slice(step, theirs).wait_recv()
    share_direct(theirs).wait_recv()
    prepare(1, g_got)
    couple(pl.ds(0, rows), 0, coupled[0])
    second_steps(2, EARLY)
    early = pl.ds(0, EARLY * CHUNK)
    couple(early, 1, coupled[1, early, :])
    for i in range(EARLY, chunks - 1):
        to_second(i).wait_recv()
        couple(at(i), 1, combine(i, 1))
    last = at(chunks - 1)
    to_second(chunks - 1).wait_recv()
    combined = combine(chunks - 1, 1)

    def partial(j, base):
        there = pl.ds(pl.multiple_of(base, CHUNK), rows)
        return dot(cols[which_mode[0], there, :], coupled[0, :, j]) + dot(
            cols[which_mode[1], there, :], coupled[1, :, j]
        )

    edges = [0, 128, 384, 640, 768, 896]
    pieces = [slice(a, b) for a, b in zip(edges, edges[1:])]
    for k, j in enumerate(pieces):
        coupled[1, last, j] = dot(combined, turned[which_mode[1], :, j]).astype(BF16)
        p_out[:, j] = partial(j, (1 - m) * rows)
        to_partner(k, j).start()
    for j in pieces:
        o_ref[0, :, j] = partial(j, m * rows) * 0.5
    @pl.loop(0, chunks)
    def _(i):
        to_second(i).wait_send()
        to_sibling(i).wait_send()

    for i in range(chunks):
        if i != SENT:
            to_first(i).wait_send()
    own_to_sibling.wait_send()
    slice_across.wait_send()
    occ_copy.wait_send()
    direct_across.wait_send()
    for step in range(ALONG_X - 1):
        ring_copy(step).wait_send()
    for step in range(ALONG_X):
        share_slice(step, half).wait_send()
    share_direct(half).wait_send()

    for k, j in enumerate(pieces):
        to_partner(k, j).wait_send()
        to_partner(k, j).wait_recv()
        o_ref[0, :, j] = o_ref[0, :, j] + p_in[:, j] * 0.5


def shards(energies, spectral, coupling, offsets, occupation):
    _, rows, norb = spectral.shape
    chunks = rows // CHUNK
    dma = pltpu.SemaphoreType.DMA
    scalar = pl.BlockSpec(memory_space=pltpu.SMEM)
    in_hbm = pl.BlockSpec(memory_space=pltpu.HBM)
    return pl.pallas_call(
        functools.partial(kernel, energies),
        out_shape=jax.ShapeDtypeStruct(spectral.shape, F32),
        in_specs=[in_hbm, in_hbm, scalar, scalar],
        out_specs=pl.BlockSpec(memory_space=pltpu.VMEM),
        scratch_shapes=[
            pltpu.VMEM((4, rows, norb), F32),
            pltpu.VMEM((norb, norb), BF16),
            pltpu.VMEM((rows - (ALONG_X - 1) * CHUNK, norb), F32),
            pltpu.VMEM((norb, norb), F32),
            pltpu.VMEM((2, norb, norb), BF16),
            pltpu.VMEM((2, norb, rows), BF16),
            pltpu.VMEM((2, rows, norb), BF16),
            pltpu.VMEM((rows, norb), F32),
            pltpu.VMEM((rows, norb), F32),
            pltpu.VMEM((8, 128), F32),
            pltpu.VMEM((8, 128), F32),
            dma,
            dma((2, chunks)),
            dma((2, chunks)),
            dma((chunks,)),
            dma((chunks,)),
            dma,
            dma,
            dma((10,)),
            dma((10,)),
            dma,
            dma,
            dma((5,)),
            dma((5,)),
        ],
        compiler_params=pltpu.CompilerParams(
            collective_id=0, has_side_effects=True, vmem_limit_bytes=48 << 20
        ),
        name="born_step",
    )(*(pltpu.with_memory_space_constraint(a, pltpu.HBM) for a in (spectral, coupling)), offsets, occupation)


def solution(mesh):
    return jax.shard_map(
        functools.partial(shards, mesh.shape["energy"]),
        mesh=mesh,
        in_specs=(P("energy", "mode", None), P("mode", None, None), P("mode"), P("mode", "energy")),
        out_specs=P("energy", "mode", None),
        check_vma=False,
    )
```

```python
import functools

import jax
import jax.numpy as jnp
from jax import lax
from jax.experimental import pallas as pl
from jax.experimental.pallas import tpu as pltpu
from jax.sharding import PartitionSpec as P

MESH = pl.DeviceIdType.MESH
CORES, ALONG_Z, ALONG_X = 2, 8, 4
CHUNK = 64
LANES = 128
PIECE = 256
EARLY = 5
SENT = 3
F32, BF16 = jnp.float32, jnp.bfloat16


def dot(a, b):
    return jnp.dot(a, b, preferred_element_type=F32)


def kernel(
    energies,
    x_ref,
    g_ref,
    off_ref,
    occ_ref,
    o_ref,
    near,
    g_mine,
    g_send_buf,
    g_got,
    turned,
    cols,
    coupled,
    p_out,
    p_in,
    occ_mine,
    occ_got,
    load_sem,
    near_send,
    near_recv,
    fwd_send,
    fwd_recv,
    sib_send,
    sib_recv,
    g_send,
    g_recv,
    occ_send,
    occ_recv,
    p_send,
    p_recv,
):
    e = lax.axis_index("energy")
    m = lax.axis_index("mode")
    rows, norb = x_ref.shape[1], x_ref.shape[2]
    chunks = rows // CHUNK
    core = e % CORES
    x_at = (e // (CORES * ALONG_Z)) % ALONG_X
    first = (lax.rem(e + energies - 2 + 4 * core, energies), m)
    second = (lax.rem(e + energies + 2 - 4 * core, energies), m)
    sibling = (e + 1 - 2 * core, m)
    partner = (e, 1 - m)
    across = (lax.rem(e + energies // 2, energies), 1 - m)
    z_at = (e // CORES) % ALONG_Z
    way = jnp.where(z_at < ALONG_Z // 2, -1, 1)
    x_next = lax.rem(x_at + way + ALONG_X, ALONG_X)
    x_last = lax.rem(x_at - way + ALONG_X, ALONG_X)
    ring_next = (e + (x_next - x_at) * (CORES * ALONG_Z), m)
    ring_last = (e + (x_last - x_at) * (CORES * ALONG_Z), m)

    load = pltpu.make_async_copy(g_ref.at[0], g_mine, load_sem)
    load.start()
    barrier = pltpu.get_barrier_semaphore()
    greeted = [first, second, sibling, partner, across, ring_last]
    for device in greeted:
        pl.semaphore_signal(barrier, inc=1, device_id=device, device_id_type=MESH)
    pl.semaphore_wait(barrier, len(greeted))

    def remote(src, dst, send, recv, device):
        return pltpu.make_async_remote_copy(
            src_ref=src, dst_ref=dst, send_sem=send, recv_sem=recv, device_id=device, device_id_type=MESH
        )

    def at(i, base=0):
        return pl.ds(pl.multiple_of(base + i * CHUNK, CHUNK), CHUNK)

    def rows_at(start):
        return pl.ds(pl.multiple_of(start, CHUNK), CHUNK)

    def to_first(i):
        return remote(x_ref.at[0, at(i)], near.at[0, at(i)], near_send.at[0, i], near_recv.at[0, i], first)

    def to_second(i):
        return remote(x_ref.at[0, at(i)], near.at[1, at(i)], near_send.at[1, i], near_recv.at[1, i], second)

    def to_sibling(i):
        return remote(near.at[0, at(i)], near.at[3, at(i)], fwd_send.at[i], fwd_recv.at[i], sibling)

    def to_partner(k, j):
        return remote(p_out.at[:, j], p_in.at[:, j], p_send.at[k], p_recv.at[k], partner)

    own_to_sibling = remote(x_ref.at[0], near.at[2], sib_send, sib_recv, sibling)

    @pl.loop(0, chunks)
    def _(i):
        to_first(i).start()

    own_to_sibling.start()

    load.wait()
    half = core * rows
    mine = half + x_at * CHUNK
    g_send_buf[0:CHUNK, :] = g_mine[rows_at(mine), :].astype(F32)
    slice_across = remote(
        g_send_buf.at[pl.ds(0, CHUNK)], g_got.at[rows_at(mine)], g_send.at[0], g_recv.at[0], across
    )
    slice_across.start()
    occ_mine[...] = jnp.full(occ_mine.shape, occ_ref[0, 0].astype(F32), F32)
    occ_copy = remote(occ_mine, occ_got, occ_send, occ_recv, partner)
    occ_copy.start()
    ring_rows = ALONG_X * CHUNK
    direct_rows = rows - ring_rows
    direct = pl.ds(pl.multiple_of(half + ring_rows, CHUNK), direct_rows)
    g_send_buf[CHUNK:, :] = g_mine[direct, :].astype(F32)
    direct_across = remote(
        g_send_buf.at[pl.ds(CHUNK, direct_rows)], g_got.at[direct], g_send.at[1], g_recv.at[1], across
    )
    direct_across.start()

    def prepare(which, matrix):
        @pl.loop(0, norb // LANES)
        def _(i):
            block = pl.ds(pl.multiple_of(i * LANES, LANES), LANES)
            turned[which, :, block] = matrix[block, :].astype(F32).T.astype(BF16)

        own = pl.ds(pl.multiple_of(m * rows, CHUNK), rows)
        cols[which] = turned[which, own, :].astype(F32).T.astype(BF16)

    prepare(0, g_mine)

    occ_copy.wait_recv()
    own_occ = occ_mine[0:1, 0:1]
    other_occ = occ_got[0:1, 0:1]
    own_one = off_ref[0] == 1
    occ_one = jnp.where(own_one, own_occ, other_occ)
    occ_two = jnp.where(own_one, other_occ, own_occ)
    low2 = jnp.where(e >= 2, 1.0, 0.0)
    high2 = jnp.where(e < energies - 2, 1.0, 0.0)
    on_core = core.astype(F32)
    ends = jnp.where((e > 0) & (e < energies - 1), 1.0, 0.0)
    which_mode = (jnp.where(own_one, 0, 1), jnp.where(own_one, 1, 0))
    from_below = (occ_two + 1.0) * low2
    from_above = occ_two * high2
    weights = (
        jnp.where(core == 0, from_above, from_below),
        jnp.where(core == 0, from_below, from_above),
        occ_one + on_core,
        (occ_one + (1.0 - on_core)) * ends,
    )

    own_to_sibling.wait_recv()

    def combine(i, which):
        a, b = (2, 3) if which == 0 else (0, 1)
        return (weights[a] * near[a, at(i), :] + weights[b] * near[b, at(i), :]).astype(BF16)

    def couple(there, which, combined):
        coupled[which, there, :] = dot(combined, turned[which_mode[which]]).astype(BF16)

    def ring_slice(step, base):
        behind = x_at - way * step + ALONG_X
        return rows_at(base + lax.rem(behind, ALONG_X) * CHUNK)

    def ring_copy(step):
        there = ring_slice(step, half)
        return remote(g_got.at[there], g_got.at[there], g_send.at[2 + step], g_recv.at[2 + step], ring_next)

    def ring_arrival(step):
        there = ring_slice(step, half)
        return remote(
            g_got.at[there], g_got.at[there], g_send.at[1 + step], g_recv.at[1 + step], ring_next
        )

    def share_slice(step, base):
        there = ring_slice(step, base)
        return remote(g_got.at[there], g_got.at[there], g_send.at[5 + step], g_recv.at[5 + step], sibling)

    def share_direct(base):
        there = pl.ds(pl.multiple_of(base + ring_rows, CHUNK), direct_rows)
        return remote(g_got.at[there], g_got.at[there], g_send.at[9], g_recv.at[9], sibling)

    def first_steps(start, stop):
        @pl.loop(start, stop)
        def _(i):
            to_first(i).wait_recv()
            to_sibling(i).start()
            to_sibling(i).wait_recv()
            coupled[0, at(i), :] = combine(i, 0)

    def second_step(i):
        to_second(i).wait_recv()
        coupled[1, at(i), :] = combine(i, 1)

    def second_steps(start, stop):
        pl.loop(start, stop)(second_step)

    slice_across.wait_recv()
    ring_copy(0).start()
    share_slice(0, half).start()
    first_steps(0, 3)
    to_first(SENT).wait_send()

    @pl.loop(0, chunks)
    def _(i):
        to_second(i).start()

    ring_arrival(1).wait_recv()
    ring_copy(1).start()
    share_slice(1, half).start()
    first_steps(3, 5)
    ring_arrival(2).wait_recv()
    ring_copy(2).start()
    share_slice(2, half).start()
    first_steps(5, chunks)
    direct_across.wait_recv()
    share_direct(half).start()
    ring_arrival(3).wait_recv()
    share_slice(3, half).start()
    second_steps(0, 2)
    theirs = (1 - core) * rows
    for step in range(ALONG_X):
        share_slice(step, theirs).wait_recv()
    share_direct(theirs).wait_recv()
    prepare(1, g_got)
    couple(pl.ds(0, rows), 0, coupled[0])
    second_steps(2, EARLY)
    early = pl.ds(0, EARLY * CHUNK)
    couple(early, 1, coupled[1, early, :])
    for i in range(EARLY, chunks - 1):
        to_second(i).wait_recv()
        couple(at(i), 1, combine(i, 1))
    last = at(chunks - 1)
    to_second(chunks - 1).wait_recv()
    combined = combine(chunks - 1, 1)

    def partial(j, base):
        there = pl.ds(pl.multiple_of(base, CHUNK), rows)
        return dot(cols[which_mode[0], there, :], coupled[0, :, j]) + dot(
            cols[which_mode[1], there, :], coupled[1, :, j]
        )

    edges = [0, 128, 384, 640, 768, 896]
    pieces = [slice(a, b) for a, b in zip(edges, edges[1:])]
    for k, j in enumerate(pieces):
        coupled[1, last, j] = dot(combined, turned[which_mode[1], :, j]).astype(BF16)
        p_out[:, j] = partial(j, (1 - m) * rows)
        to_partner(k, j).start()
    for j in pieces:
        o_ref[0, :, j] = partial(j, m * rows) * 0.5
    @pl.loop(0, chunks)
    def _(i):
        to_second(i).wait_send()
        to_sibling(i).wait_send()

    for i in range(chunks):
        if i != SENT:
            to_first(i).wait_send()
    own_to_sibling.wait_send()
    slice_across.wait_send()
    occ_copy.wait_send()
    direct_across.wait_send()
    for step in range(ALONG_X - 1):
        ring_copy(step).wait_send()
    for step in range(ALONG_X):
        share_slice(step, half).wait_send()
    share_direct(half).wait_send()

    for k, j in enumerate(pieces):
        to_partner(k, j).wait_send()
        to_partner(k, j).wait_recv()
        o_ref[0, :, j] = o_ref[0, :, j] + p_in[:, j] * 0.5


def shards(energies, spectral, coupling, offsets, occupation):
    _, rows, norb = spectral.shape
    chunks = rows // CHUNK
    dma = pltpu.SemaphoreType.DMA
    scalar = pl.BlockSpec(memory_space=pltpu.SMEM)
    in_hbm = pl.BlockSpec(memory_space=pltpu.HBM)
    return pl.pallas_call(
        functools.partial(kernel, energies),
        out_shape=jax.ShapeDtypeStruct(spectral.shape, F32),
        in_specs=[in_hbm, in_hbm, scalar, scalar],
        out_specs=pl.BlockSpec(memory_space=pltpu.VMEM),
        scratch_shapes=[
            pltpu.VMEM((4, rows, norb), F32),
            pltpu.VMEM((norb, norb), BF16),
            pltpu.VMEM((rows - (ALONG_X - 1) * CHUNK, norb), F32),
            pltpu.VMEM((norb, norb), F32),
            pltpu.VMEM((2, norb, norb), BF16),
            pltpu.VMEM((2, norb, rows), BF16),
            pltpu.VMEM((2, rows, norb), BF16),
            pltpu.VMEM((rows, norb), F32),
            pltpu.VMEM((rows, norb), F32),
            pltpu.VMEM((8, 128), F32),
            pltpu.VMEM((8, 128), F32),
            dma,
            dma((2, chunks)),
            dma((2, chunks)),
            dma((chunks,)),
            dma((chunks,)),
            dma,
            dma,
            dma((10,)),
            dma((10,)),
            dma,
            dma,
            dma((5,)),
            dma((5,)),
        ],
        compiler_params=pltpu.CompilerParams(
            collective_id=0, has_side_effects=True, vmem_limit_bytes=48 << 20
        ),
        name="born_step",
    )(*(pltpu.with_memory_space_constraint(a, pltpu.HBM) for a in (spectral, coupling)), offsets, occupation)


def solution(mesh):
    return jax.shard_map(
        functools.partial(shards, mesh.shape["energy"]),
        mesh=mesh,
        in_specs=(P("energy", "mode", None), P("mode", None, None), P("mode"), P("mode", "energy")),
        out_specs=P("energy", "mode", None),
        check_vma=False,
    )
```
